512 devices in a mesh: row: 64 (over x, z, core), blk: 8 (over y).
Axes of the slice: x: 4, y: 8, z: 8, core: 2. Of those that a mesh axis runs over, the one named last changes fastest.
Arguments:
- factor_panel: bfloat16 [131072, 2, 2048], P('row', None, 'blk'), may hold values from -0.09375 to 0.09375
- right_side: float32 [256, 131072], P('blk', 'row'), may hold values from -6 to 6
- block_inverse: float32 [2, 2048, 2048], P(None, 'row', 'blk'), may hold values from -2 to 2, as said below
Outputs:
- solved: float32 [2, 256, 2048], P(None, 'blk', 'row')
- reduced_side: float32 [256, 131072], P('blk', 'row')
The draws below stay inside these ranges and needn't reach their ends.
Inputs may be any that keep to these rules, and one draw needn't show every extreme that they name: block_inverse[k] is lower triangular with diagonal entries between 1 and 2.
All inputs are finite; a program needn't handle non-finite values.
Results may differ from the reference program's by a relative error of at most 0.015.
Values may be sent and summed in bfloat16 or wider, within the bound.
No kernel may reach another device: no remote copies, remote signals or barrier semaphores. Data moves between devices by JAX's collectives and lax.ppermute only.
A program may use at most 64 MiB of HBM per device.

```python
import jax
import jax.numpy as jnp
from jax import lax

NB = 2048
STEPS = 2
DATES = 256
ORDER = 131072
N_BLK = 8


def draw_block_inverse(key, part):
    key_off = jax.random.fold_in(key, 11)
    key_diag = jax.random.fold_in(key, 12)
    scale = 0.5 / NB ** 0.5
    lower = jnp.clip(jax.random.normal(key_off, (STEPS, NB, NB), jnp.float32), -4.0, 4.0) * scale
    diag = jax.random.uniform(key_diag, (STEPS, NB, NB), jnp.float32, 1.0, 2.0)
    rows = jnp.arange(NB)[:, None]
    cols = jnp.arange(NB)[None, :]
    return jnp.where(rows > cols, lower, jnp.where(rows == cols, diag, jnp.float32(0.0)))


def shard_levels(key, shape, cuts, least, largest):
    def one(position, shards_of):
        draws = jax.random.uniform(jax.random.fold_in(jax.random.fold_in(key, 6), position), (shards_of,), jnp.float32, least / len(cuts), largest / len(cuts))
        return jnp.repeat(jnp.exp(draws), shape[position] // shards_of).reshape((-1,) + (1,) * (len(shape) - position - 1))

    level = one(*cuts[0])
    for cut in cuts[1:]:
        level = level * one(*cut)
    return level


def noise(rng, extent, deviation, bound, cuts=(), kind=jnp.bfloat16):
    array = jax.random.normal(rng, extent, jnp.float32) * deviation
    if len(cuts) > 0:
        array = shard_levels(rng, extent, cuts, -0.22, 0.18) * array
    return jnp.clip(array, min=-bound, max=bound).astype(kind)


def setup_inputs(seed: int = 0) -> dict:
    seeds = jax.random.split(jax.random.key(seed), 4)
    factor_panel = noise(seeds[0], (ORDER, STEPS, NB), (2 * NB) ** -0.5, 0.09375, ((0, 64), (2, 8)))
    right_side = noise(seeds[1], (DATES, ORDER), 1.0, 6.0, ((0, 8), (1, 64)), jnp.float32)
    block_inverse = draw_block_inverse(jax.random.fold_in(seeds[3], 71), 0)
    return dict(factor_panel=factor_panel, right_side=right_side, block_inverse=block_inverse)


def reference(factor_panel, right_side, block_inverse):
    reduced_side = right_side
    column_index = jnp.arange(ORDER, dtype=jnp.int32)
    width = NB // N_BLK
    outputs = []
    for section in range(STEPS):
        pivot_rows = lax.dynamic_slice_in_dim(reduced_side, section * NB, NB, 1)
        solved_now = jnp.dot(pivot_rows, block_inverse[section].T, precision=lax.Precision.HIGHEST)
        outputs.append(solved_now)
        solved_half = solved_now.astype(jnp.bfloat16).astype(jnp.float32)
        panel_now = factor_panel[:, section, :].astype(jnp.float32)
        update = jnp.zeros((DATES, ORDER), jnp.float32)
        for group in range(N_BLK):
            left = solved_half[:, group * width:(group + 1) * width]
            right = panel_now[:, group * width:(group + 1) * width]
            term = jnp.dot(left, right.T, precision=lax.Precision.HIGHEST)
            term = lax.optimization_barrier(term.astype(jnp.bfloat16))
            update = update + term.astype(jnp.float32)
        below = (column_index >= (section + 1) * NB)[None, :]
        reduced_side = reduced_side - jnp.where(below, update, jnp.float32(0.0))
    return jnp.stack(outputs), reduced_side
```

```python
import jax
import jax.numpy as jnp
from jax import lax
from jax.sharding import Mesh, PartitionSpec as P


STEPS = 2
NX, NZ, NC = 4, 8, 2
HALF = jnp.bfloat16
WIDE = jnp.float32


def swap_blocks(array, axis):
    return lax.all_to_all(array, axis, split_axis=0, concat_axis=0, tiled=True)


def gather_by_swap(array, axis, count):
    return swap_blocks(jnp.broadcast_to(array[None], (count, *array.shape)), axis)


def product(left, right):
    return lax.dot_general(left, right, (((1,), (1,)), ((), ())), preferred_element_type=WIDE)


def scatter_sum(partial, blocks):
    t, wide = partial.shape
    split = partial.astype(HALF).reshape(t, blocks, wide // blocks).transpose(1, 0, 2)
    return jnp.sum(swap_blocks(split, "blk").astype(WIDE), axis=0)


def local(factor_panel, right_side, block_inverse):
    x = lax.axis_index("x")
    z = lax.axis_index("z")
    core = lax.axis_index("core")
    blk = lax.axis_index("blk")
    row = (x * NZ + z) * NC + core
    n_blk = right_side.shape[1] // factor_panel.shape[2]
    pixels, _, width = factor_panel.shape
    dates_local = right_side.shape[0]
    dates_x = dates_local // NX
    t = dates_x * n_blk
    rows_local = block_inverse.shape[1]
    per_blk = width // rows_local
    half = width // NC

    first_panel = factor_panel[:, 0, :]

    pivot = right_side.astype(HALF).reshape(NX, dates_x, pixels)
    mine = jnp.where(x == 0, pivot[0], jnp.zeros_like(pivot[0]))
    for k in range(1, NX):
        mine = mine + lax.ppermute(pivot[k], ("x", "z"), [(0, k * NZ)])

    halves = first_panel.reshape(n_blk, NC, half, width).transpose(1, 0, 2, 3)
    sent = lax.ppermute(halves[0], ("x", "z", "core"), [(1, 0)])
    lower = jnp.where(core == 1, halves[1], sent)
    cross = jnp.where((x == 0) & (z == 0), lower, jnp.zeros_like(lower))
    for k in range(1, NX):
        cross = cross + lax.ppermute(lower, ("x", "z"), [(0, k * NZ)])
    cross = cross.reshape(n_blk * half, width)

    inverse = gather_by_swap(block_inverse.astype(HALF), "x", NX)
    planes = [inverse] + [lax.ppermute(inverse, "z", [(k, 0)]) for k in range(1, NZ)]
    inverse = jnp.stack(planes).transpose(2, 1, 0, 3, 4)
    inverse = inverse.reshape(STEPS, NX * NZ * rows_local, width)

    pivot = swap_blocks(mine.reshape(dates_x, n_blk, width).transpose(1, 0, 2), "blk")
    pivot = lax.all_gather(pivot.reshape(t, width), "core", axis=0, tiled=False)

    place = jnp.arange(width)
    c_of, q_of, i_of = place // half, place % half // rows_local, place % rows_local
    natural = (q_of * NC + c_of) * rows_local + i_of
    order = (natural[:, None] == place[None, :]).astype(HALF)

    def ordered(value):
        return jnp.dot(value, order, preferred_element_type=WIDE).astype(HALF)

    def both_cores(value):
        pair = lax.all_gather(value, "core", axis=0, tiled=False)
        return jnp.concatenate([pair[0], pair[1]], axis=-1)

    first = scatter_sum(product(pivot[0], inverse[0]), n_blk).astype(HALF)
    update = scatter_sum(product(ordered(both_cores(first)), cross), n_blk)
    reduced = pivot[1].astype(WIDE) - both_cores(update)
    second = scatter_sum(product(reduced.astype(HALF), inverse[1]), n_blk).astype(HALF)

    solved = jnp.stack([first, second])
    spread = jnp.where(z == 0, solved, jnp.zeros_like(solved))
    for k in range(1, NZ):
        spread = spread + lax.ppermute(solved, "z", [(0, k)])
    spread = ordered(both_cores(gather_by_swap(spread, "x", NX)))
    spread = spread.reshape(NX, STEPS, n_blk, dates_x, width).transpose(2, 0, 3, 1, 4)
    spread = spread.reshape(dates_local * n_blk, STEPS * width)

    panel = jnp.concatenate(
        [
            jnp.where(row > k, factor_panel[:, k, :], jnp.zeros((), HALF))
            for k in range(STEPS)
        ],
        axis=1,
    )
    extra = 128
    pick = jnp.arange(extra)
    at = pick // rows_local * width + row % per_blk * rows_local + pick % rows_local
    wanted = (pick < STEPS * rows_local) & (row // per_blk == blk)
    select = wanted[:, None] & (at[:, None] == jnp.arange(STEPS * width)[None, :])
    panel = jnp.concatenate([panel, select.astype(HALF)], axis=0)

    total = product(spread, panel).astype(HALF).reshape(n_blk, dates_local, pixels + extra)
    total = jnp.sum(swap_blocks(total, "blk").astype(WIDE), axis=0)
    answer = total[:, pixels : pixels + STEPS * rows_local]
    answer = answer.reshape(dates_local, STEPS, rows_local).transpose(1, 0, 2)
    return (answer, right_side - total[:, :pixels])


def solution(mesh):
    shape = (NX, NZ, NC, mesh.shape["blk"])
    fine = Mesh(mesh.devices.reshape(shape), ("x", "z", "core", "blk"))
    row = ("x", "z", "core")
    return jax.shard_map(
        local,
        mesh=fine,
        in_specs=(P(row, None, "blk"), P("blk", row), P(None, row, "blk")),
        out_specs=(P(None, "blk", row), P("blk", row)),
        check_vma=False,
    )
```

```python
import jax
import jax.numpy as jnp
from jax import lax
from jax.sharding import Mesh, PartitionSpec as P


STEPS = 2
NX, NZ, NC = 4, 8, 2
HALF = jnp.bfloat16
WIDE = jnp.float32


def swap_blocks(array, axis):
    return lax.all_to_all(array, axis, split_axis=0, concat_axis=0, tiled=True)


def gather_by_swap(array, axis, count):
    return swap_blocks(jnp.broadcast_to(array[None], (count, *array.shape)), axis)


def product(left, right):
    return lax.dot_general(left, right, (((1,), (1,)), ((), ())), preferred_element_type=WIDE)


def scatter_sum(partial, blocks):
    t, wide = partial.shape
    split = partial.astype(HALF).reshape(t, blocks, wide // blocks).transpose(1, 0, 2)
    return jnp.sum(swap_blocks(split, "blk").astype(WIDE), axis=0)


def local(factor_panel, right_side, block_inverse):
    x = lax.axis_index("x")
    z = lax.axis_index("z")
    core = lax.axis_index("core")
    blk = lax.axis_index("blk")
    row = (x * NZ + z) * NC + core
    n_blk = right_side.shape[1] // factor_panel.shape[2]
    pixels, _, width = factor_panel.shape
    dates_local = right_side.shape[0]
    dates_x = dates_local // NX
    t = dates_x * n_blk
    rows_local = block_inverse.shape[1]
    per_blk = width // rows_local
    half = width // NC

    pivot = right_side.astype(HALF).reshape(NX, dates_x, pixels)
    mine = jnp.where(x == 0, pivot[0], jnp.zeros_like(pivot[0]))
    for k in range(1, NX):
        mine = mine + lax.ppermute(pivot[k], ("x", "z"), [(0, k * NZ)])

    inverse = gather_by_swap(block_inverse.astype(HALF), "x", NX)
    planes = [inverse] + [lax.ppermute(inverse, "z", [(k, 0)]) for k in range(1, NZ)]
    inverse = jnp.stack(planes).transpose(2, 1, 0, 3, 4)
    inverse = inverse.reshape(STEPS, NX * NZ * rows_local, width)

    pivot = swap_blocks(mine.reshape(dates_x, n_blk, width).transpose(1, 0, 2), "blk")
    pivot = lax.all_gather(pivot.reshape(t, width), "core", axis=0, tiled=False)

    panels = factor_panel.transpose(1, 0, 2)
    halves = panels[0].reshape(n_blk, NC, half, width)
    sent = lax.ppermute(halves[:, 0], ("x", "z", "core"), [(1, 0)])
    lower = jnp.where(core == 1, halves[:, 1], sent)
    cross = jnp.where((x == 0) & (z == 0), lower, jnp.zeros_like(lower))
    for k in range(1, NX):
        cross = cross + lax.ppermute(lower, ("x", "z"), [(0, k * NZ)])
    cross = cross.reshape(n_blk * half, width)

    place = jnp.arange(width)
    c_of, q_of, i_of = place // half, place % half // rows_local, place % rows_local
    natural = (q_of * NC + c_of) * rows_local + i_of
    order = (natural[:, None] == place[None, :]).astype(HALF)

    def ordered(value):
        return jnp.dot(value, order, preferred_element_type=WIDE).astype(HALF)

    def both_cores(value):
        pair = lax.all_gather(value, "core", axis=0, tiled=False)
        return jnp.concatenate([pair[0], pair[1]], axis=-1)

    first = scatter_sum(product(pivot[0], inverse[0]), n_blk).astype(HALF)
    first, panels = lax.optimization_barrier((first, panels))
    update = scatter_sum(product(ordered(both_cores(first)), cross), n_blk)
    reduced = pivot[1].astype(WIDE) - both_cores(update)
    second = scatter_sum(product(reduced.astype(HALF), inverse[1]), n_blk).astype(HALF)

    solved = jnp.stack([first, second])
    spread = jnp.where(z == 0, solved, jnp.zeros_like(solved))
    for k in range(1, NZ):
        spread = spread + lax.ppermute(solved, "z", [(0, k)])
    spread = ordered(both_cores(gather_by_swap(spread, "x", NX)))
    spread = spread.reshape(NX, STEPS, n_blk, dates_x, width).transpose(2, 0, 3, 1, 4)
    spread = spread.reshape(dates_local * n_blk, STEPS * width)

    panel = jnp.concatenate(
        [
            jnp.where(row > k, panels[k], jnp.zeros((), HALF))
            for k in range(STEPS)
        ],
        axis=1,
    )
    extra = 128
    pick = jnp.arange(extra)
    at = pick // rows_local * width + row % per_blk * rows_local + pick % rows_local
    wanted = (pick < STEPS * rows_local) & (row // per_blk == blk)
    select = wanted[:, None] & (at[:, None] == jnp.arange(STEPS * width)[None, :])
    panel = jnp.concatenate([panel, select.astype(HALF)], axis=0)

    total = product(spread, panel).astype(HALF)
    lanes, rows8 = 128, 8
    total = total.reshape(n_blk * dates_local // rows8, rows8, -1, lanes).transpose(0, 2, 1, 3)
    total = swap_blocks(total.reshape(n_blk, -1, lanes), "blk")
    total = jnp.sum(total.astype(WIDE), axis=0)
    total = total.reshape(dates_local // rows8, -1, rows8, lanes).transpose(0, 2, 1, 3)
    total = total.reshape(dates_local, pixels + extra)
    answer = total[:, pixels : pixels + STEPS * rows_local]
    answer = answer.reshape(dates_local, STEPS, rows_local).transpose(1, 0, 2)
    return (answer, right_side - total[:, :pixels])


def solution(mesh):
    shape = (NX, NZ, NC, mesh.shape["blk"])
    fine = Mesh(mesh.devices.reshape(shape), ("x", "z", "core", "blk"))
    row = ("x", "z", "core")
    return jax.shard_map(
        local,
        mesh=fine,
        in_specs=(P(row, None, "blk"), P("blk", row), P(None, row, "blk")),
        out_specs=(P(None, "blk", row), P("blk", row)),
        check_vma=False,
    )
```

```python
import jax
import jax.numpy as jnp
from jax import lax
from jax.experimental import pallas as pl
from jax.experimental.pallas import tpu as pltpu
from jax.sharding import Mesh, PartitionSpec as P


STEPS = 2
NX, NZ, NC = 4, 8, 2
HALF = jnp.bfloat16
WIDE = jnp.float32


def swap_blocks(array, axis):
    return lax.all_to_all(array, axis, split_axis=0, concat_axis=0, tiled=True)


def gather_by_swap(array, axis, count):
    return swap_blocks(jnp.broadcast_to(array[None], (count, *array.shape)), axis)


def product(left, right):
    return lax.dot_general(left, right, (((1,), (1,)), ((), ())), preferred_element_type=WIDE)


def scatter_sum(split):
    return jnp.sum(swap_blocks(split, "blk").astype(WIDE), axis=0)


def assemble(planes, whole):
    for z, plane in enumerate(planes):
        count, size, _ = plane.shape
        for x in range(count):
            at = (x * len(planes) + z) * size
            whole[at : at + size, :] = plane[x]


def write_blocks(value, whole, out):
    size = out.shape[2]
    for g in range(out.shape[0]):
        out[g] = product(value, whole[g * size : (g + 1) * size, :]).astype(out.dtype)


def first_kernel(pivot, *refs):
    planes, (out, whole) = refs[:NZ], refs[NZ:]
    assemble(planes, whole)
    write_blocks(pivot[...], whole, out)


def cross_kernel(pair, order, own, *refs):
    others, (out, whole) = refs[: NX - 1], refs[NX - 1 :]
    value = product(pair[0], order[0])
    for c in range(1, NC):
        value = value + product(pair[c], order[c])
    blocks, size, _ = own.shape
    for g in range(blocks):
        whole[g * size : (g + 1) * size, :] = own[g]
        for other in others:
            whole[g * size : (g + 1) * size, :] += other[g]
    write_blocks(value.astype(HALF), whole, out)


def second_kernel(pivot, update, *refs):
    planes, (out, whole, value) = refs[:NZ], refs[NZ:]
    assemble(planes, whole)
    half = update.shape[2]
    for c in range(NC):
        part = pivot[:, c * half : (c + 1) * half].astype(WIDE) - update[c]
        value[:, c * half : (c + 1) * half] = part.astype(HALF)
    write_blocks(value[...], whole, out)


def run_kernel(kernel, blocks, t, size, width, scratch, *operands):
    return pl.pallas_call(
        kernel,
        out_shape=jax.ShapeDtypeStruct((blocks, t, size), HALF),
        scratch_shapes=[pltpu.VMEM((blocks * size, width), HALF), *scratch],
    )(*operands)


def local(factor_panel, right_side, block_inverse):
    x = lax.axis_index("x")
    z = lax.axis_index("z")
    core = lax.axis_index("core")
    blk = lax.axis_index("blk")
    row = (x * NZ + z) * NC + core
    n_blk = right_side.shape[1] // factor_panel.shape[2]
    pixels, _, width = factor_panel.shape
    dates_local = right_side.shape[0]
    dates_x = dates_local // NX
    t = dates_x * n_blk
    rows_local = block_inverse.shape[1]
    per_blk = width // rows_local
    half = width // NC

    pivot = right_side.astype(HALF).reshape(NX, dates_x, pixels)
    mine = jnp.where(x == 0, pivot[0], jnp.zeros_like(pivot[0]))
    for k in range(1, NX):
        mine = mine + lax.ppermute(pivot[k], ("x", "z"), [(0, k * NZ)])

    inverse = gather_by_swap(block_inverse.astype(HALF), "x", NX)
    pivot = swap_blocks(mine.reshape(dates_x, n_blk, width).transpose(1, 0, 2), "blk")
    pivot = lax.all_gather(pivot.reshape(t, width), "core", axis=0, tiled=False)

    panels = factor_panel.transpose(1, 0, 2)
    halves = panels[0].reshape(n_blk, NC, half, width)
    sent = lax.ppermute(halves[:, 0], ("x", "z", "core"), [(1, 0)])
    lower = jnp.where(core == 1, halves[:, 1], sent)
    cross = [jnp.where((x == 0) & (z == 0), lower, jnp.zeros_like(lower))]
    cross += [lax.ppermute(lower, ("x", "z"), [(0, k * NZ)]) for k in range(1, NX)]

    place = jnp.arange(width)
    c_of, q_of, i_of = place // half, place % half // rows_local, place % rows_local
    natural = (q_of * NC + c_of) * rows_local + i_of
    order = (natural[:, None] == place[None, :]).astype(HALF)
    pair_order = order.reshape(NC, half, width).transpose(0, 2, 1)
    sizes = (n_blk, t, half, width)

    def planes_of(k):
        mine = inverse[:, k]
        return [mine] + [lax.ppermute(mine, "z", [(source, 0)]) for source in range(1, NZ)]

    def ordered(value):
        return jnp.dot(value, order, preferred_element_type=WIDE).astype(HALF)

    def both_cores(value):
        pair = lax.all_gather(value, "core", axis=0, tiled=False)
        return jnp.concatenate([pair[0], pair[1]], axis=-1)

    planes = planes_of(0)
    partial = run_kernel(first_kernel, *sizes, (), pivot[0], *planes)
    first = scatter_sum(partial).astype(HALF)
    first, panels = lax.optimization_barrier((first, panels))
    planes = planes_of(1)
    pair = lax.all_gather(first, "core", axis=0, tiled=False)
    partial = run_kernel(cross_kernel, *sizes, (), pair, pair_order, *cross)
    update = scatter_sum(partial)
    pair = lax.all_gather(update, "core", axis=0, tiled=False)
    scratch = (pltpu.VMEM((t, width), HALF),)
    partial = run_kernel(second_kernel, *sizes, scratch, pivot[1], pair, *planes)
    second = scatter_sum(partial).astype(HALF)

    solved = jnp.stack([first, second])
    spread = jnp.where(z == 0, solved, jnp.zeros_like(solved))
    for k in range(1, NZ):
        spread = spread + lax.ppermute(solved, "z", [(0, k)])
    spread = ordered(both_cores(gather_by_swap(spread, "x", NX)))
    spread = spread.reshape(NX, STEPS, n_blk, dates_x, width).transpose(2, 0, 3, 1, 4)
    spread = spread.reshape(dates_local * n_blk, STEPS * width)

    panel = jnp.concatenate(
        [
            jnp.where(row > k, panels[k], jnp.zeros((), HALF))
            for k in range(STEPS)
        ],
        axis=1,
    )
    extra = 512
    pick = jnp.arange(extra)
    at = pick // rows_local * width + row % per_blk * rows_local + pick % rows_local
    wanted = (pick < STEPS * rows_local) & (row // per_blk == blk)
    select = wanted[:, None] & (at[:, None] == jnp.arange(STEPS * width)[None, :])
    panel = jnp.concatenate([panel, select.astype(HALF)], axis=0)

    total = product(spread, panel).astype(HALF)
    lanes, rows8 = 128, 8
    total = total.reshape(n_blk * dates_local // rows8, rows8, -1, lanes).transpose(0, 2, 1, 3)
    total = swap_blocks(total.reshape(n_blk, -1, lanes), "blk")
    total = jnp.sum(total.astype(WIDE), axis=0)
    total = total.reshape(dates_local // rows8, -1, rows8, lanes).transpose(0, 2, 1, 3)
    total = total.reshape(dates_local, pixels + extra)
    answer = total[:, pixels : pixels + STEPS * rows_local]
    answer = answer.reshape(dates_local, STEPS, rows_local).transpose(1, 0, 2)
    return (answer, right_side - total[:, :pixels])


def solution(mesh):
    shape = (NX, NZ, NC, mesh.shape["blk"])
    fine = Mesh(mesh.devices.reshape(shape), ("x", "z", "core", "blk"))
    row = ("x", "z", "core")
    return jax.shard_map(
        local,
        mesh=fine,
        in_specs=(P(row, None, "blk"), P("blk", row), P(None, row, "blk")),
        out_specs=(P(None, "blk", row), P("blk", row)),
        check_vma=False,
    )
```

```python
import jax
import jax.numpy as jnp
from jax import lax
from jax.experimental import pallas as pl
from jax.experimental.pallas import tpu as pltpu
from jax.sharding import Mesh, PartitionSpec as P


STEPS = 2
NX, NZ, NC = 4, 8, 2
HALF = jnp.bfloat16
WIDE = jnp.float32


def swap_blocks(array, axis):
    return lax.all_to_all(array, axis, split_axis=0, concat_axis=0, tiled=True)


def gather_by_swap(array, axis, count):
    return swap_blocks(jnp.broadcast_to(array[None], (count, *array.shape)), axis)


def product(left, right):
    return lax.dot_general(left, right, (((1,), (1,)), ((), ())), preferred_element_type=WIDE)


def scatter_sum(split):
    return jnp.sum(swap_blocks(split, "blk").astype(WIDE), axis=0)


def assemble(planes, step, whole):
    for z, plane in enumerate(planes):
        count, _, size, _ = plane.shape
        for x in range(count):
            at = (x * len(planes) + z) * size
            whole[at : at + size, :] = plane[x, step]


def write_blocks(value, whole, out):
    size = out.shape[2]
    for g in range(out.shape[0]):
        out[g] = product(value, whole[g * size : (g + 1) * size, :]).astype(out.dtype)


def first_kernel(pivot, *refs):
    planes, (out, whole) = refs[:NZ], refs[NZ:]
    assemble(planes, 0, whole)
    write_blocks(pivot[...], whole, out)


def cross_kernel(pair, order, own, *refs):
    others, (out, whole) = refs[: NX - 1], refs[NX - 1 :]
    value = product(pair[0], order[0])
    for c in range(1, NC):
        value = value + product(pair[c], order[c])
    blocks, size, _ = own.shape
    for g in range(blocks):
        whole[g * size : (g + 1) * size, :] = own[g]
        for other in others:
            whole[g * size : (g + 1) * size, :] += other[g]
    write_blocks(value.astype(HALF), whole, out)


def second_kernel(pivot, update, *refs):
    planes, (out, whole, value) = refs[:NZ], refs[NZ:]
    assemble(planes, 1, whole)
    half = update.shape[2]
    for c in range(NC):
        part = pivot[:, c * half : (c + 1) * half].astype(WIDE) - update[c]
        value[:, c * half : (c + 1) * half] = part.astype(HALF)
    write_blocks(value[...], whole, out)


def run_kernel(kernel, blocks, t, size, width, scratch, *operands):
    return pl.pallas_call(
        kernel,
        out_shape=jax.ShapeDtypeStruct((blocks, t, size), HALF),
        scratch_shapes=[pltpu.VMEM((blocks * size, width), HALF), *scratch],
    )(*operands)


def local(factor_panel, right_side, block_inverse):
    x = lax.axis_index("x")
    z = lax.axis_index("z")
    core = lax.axis_index("core")
    blk = lax.axis_index("blk")
    row = (x * NZ + z) * NC + core
    n_blk = right_side.shape[1] // factor_panel.shape[2]
    pixels, _, width = factor_panel.shape
    dates_local = right_side.shape[0]
    dates_x = dates_local // NX
    t = dates_x * n_blk
    rows_local = block_inverse.shape[1]
    per_blk = width // rows_local
    half = width // NC

    pivot = right_side.astype(HALF).reshape(NX, dates_x, pixels)
    mine = jnp.where(x == 0, pivot[0], jnp.zeros_like(pivot[0]))
    for k in range(1, NX):
        mine = mine + lax.ppermute(pivot[k], ("x", "z"), [(0, k * NZ)])

    inverse = gather_by_swap(block_inverse.astype(HALF), "x", NX)
    pivot = swap_blocks(mine.reshape(dates_x, n_blk, width).transpose(1, 0, 2), "blk")
    pivot = lax.all_gather(pivot.reshape(t, width), "core", axis=0, tiled=False)

    panels = factor_panel.transpose(1, 0, 2)
    halves = panels[0].reshape(n_blk, NC, half, width)
    sent = lax.ppermute(halves[:, 0], ("x", "z", "core"), [(1, 0)])
    lower = jnp.where(core == 1, halves[:, 1], sent)
    cross = [jnp.where((x == 0) & (z == 0), lower, jnp.zeros_like(lower))]
    cross += [lax.ppermute(lower, ("x", "z"), [(0, k * NZ)]) for k in range(1, NX)]

    place = jnp.arange(width)
    c_of, q_of, i_of = place // half, place % half // rows_local, place % rows_local
    natural = (q_of * NC + c_of) * rows_local + i_of
    order = (natural[:, None] == place[None, :]).astype(HALF)
    pair_order = order.reshape(NC, half, width).transpose(0, 2, 1)
    sizes = (n_blk, t, half, width)


    def ordered(value):
        return jnp.dot(value, order, preferred_element_type=WIDE).astype(HALF)

    def both_cores(value):
        pair = lax.all_gather(value, "core", axis=0, tiled=False)
        return jnp.concatenate([pair[0], pair[1]], axis=-1)

    planes = [inverse] + [lax.ppermute(inverse, "z", [(k, 0)]) for k in range(1, NZ)]
    partial = run_kernel(first_kernel, *sizes, (), pivot[0], *planes)
    first = scatter_sum(partial).astype(HALF)
    first, panels = lax.optimization_barrier((first, panels))
    pair = lax.all_gather(first, "core", axis=0, tiled=False)
    partial = run_kernel(cross_kernel, *sizes, (), pair, pair_order, *cross)
    update = scatter_sum(partial)
    pair = lax.all_gather(update, "core", axis=0, tiled=False)
    scratch = (pltpu.VMEM((t, width), HALF),)
    partial = run_kernel(second_kernel, *sizes, scratch, pivot[1], pair, *planes)
    second = scatter_sum(partial).astype(HALF)

    solved = jnp.stack([first, second])
    spread = jnp.where(z == 0, solved, jnp.zeros_like(solved))
    for k in range(1, NZ):
        spread = spread + lax.ppermute(solved, "z", [(0, k)])
    spread = ordered(both_cores(gather_by_swap(spread, "x", NX)))
    spread = spread.reshape(NX, STEPS, n_blk, dates_x, width).transpose(2, 0, 3, 1, 4)
    spread = spread.reshape(dates_local * n_blk, STEPS * width)

    panel = jnp.concatenate(
        [
            jnp.where(row > k, panels[k], jnp.zeros((), HALF))
            for k in range(STEPS)
        ],
        axis=1,
    )
    extra = 128
    pick = jnp.arange(extra)
    at = pick // rows_local * width + row % per_blk * rows_local + pick % rows_local
    wanted = (pick < STEPS * rows_local) & (row // per_blk == blk)
    select = wanted[:, None] & (at[:, None] == jnp.arange(STEPS * width)[None, :])
    panel = jnp.concatenate([panel, select.astype(HALF)], axis=0)

    total = product(spread, panel).astype(HALF)
    lanes, rows8 = 128, 8
    total = total.reshape(n_blk * dates_local // rows8, rows8, -1, lanes).transpose(0, 2, 1, 3)
    total = swap_blocks(total.reshape(n_blk, -1, lanes), "blk")
    total = jnp.sum(total.astype(WIDE), axis=0)
    total = total.reshape(dates_local // rows8, -1, rows8, lanes).transpose(0, 2, 1, 3)
    total = total.reshape(dates_local, pixels + extra)
    answer = total[:, pixels : pixels + STEPS * rows_local]
    answer = answer.reshape(dates_local, STEPS, rows_local).transpose(1, 0, 2)
    return (answer, right_side - total[:, :pixels])


def solution(mesh):
    shape = (NX, NZ, NC, mesh.shape["blk"])
    fine = Mesh(mesh.devices.reshape(shape), ("x", "z", "core", "blk"))
    row = ("x", "z", "core")
    return jax.shard_map(
        local,
        mesh=fine,
        in_specs=(P(row, None, "blk"), P("blk", row), P(None, row, "blk")),
        out_specs=(P(None, "blk", row), P("blk", row)),
        check_vma=False,
    )
```

```python
import jax
import jax.numpy as jnp
from jax import lax
from jax.experimental import pallas as pl
from jax.experimental.pallas import tpu as pltpu
from jax.sharding import Mesh, PartitionSpec as P


STEPS = 2
NX, NZ, NC = 4, 8, 2
HALF = jnp.bfloat16
WIDE = jnp.float32


def swap_blocks(array, axis):
    return lax.all_to_all(array, axis, split_axis=0, concat_axis=0, tiled=True)


def gather_by_swap(array, axis, count):
    return swap_blocks(jnp.broadcast_to(array[None], (count, *array.shape)), axis)


def product(left, right):
    return lax.dot_general(left, right, (((1,), (1,)), ((), ())), preferred_element_type=WIDE)


def scatter_sum(split):
    return jnp.sum(swap_blocks(split, "blk").astype(WIDE), axis=0)


def assemble(planes, step, whole):
    for z, plane in enumerate(planes):
        count, _, size, _ = plane.shape
        for x in range(count):
            at = (x * len(planes) + z) * size
            whole[at : at + size, :] = plane[x, step]


def write_blocks(value, whole, out):
    size = out.shape[2]
    for g in range(out.shape[0]):
        out[g] = product(value, whole[g * size : (g + 1) * size, :]).astype(out.dtype)


def first_kernel(pivot, *refs):
    planes, (out, whole) = refs[:NZ], refs[NZ:]
    assemble(planes, 0, whole)
    write_blocks(pivot[...], whole, out)


def cross_kernel(owner, pair, order, own, *refs):
    others, (out, whole) = refs[: NX - 1], refs[NX - 1 :]
    value = product(pair[0], order[0])
    for c in range(1, NC):
        value = value + product(pair[c], order[c])
    blocks, size, _ = own.shape

    @pl.when(owner[0] == 1)
    def _():
        for g in range(blocks):
            whole[g * size : (g + 1) * size, :] = own[g]

    @pl.when(owner[0] == 0)
    def _():
        for g in range(blocks):
            part = others[0][g]
            for other in others[1:]:
                part = part + other[g]
            whole[g * size : (g + 1) * size, :] = part

    write_blocks(value.astype(HALF), whole, out)


def second_kernel(pivot, update, *refs):
    planes, (out, whole, value) = refs[:NZ], refs[NZ:]
    assemble(planes, 1, whole)
    half = update.shape[2]
    for c in range(NC):
        part = pivot[:, c * half : (c + 1) * half].astype(WIDE) - update[c]
        value[:, c * half : (c + 1) * half] = part.astype(HALF)
    write_blocks(value[...], whole, out)


def run_kernel(kernel, blocks, t, size, width, scratch, *operands):
    spaces = [pltpu.SMEM if item.dtype == jnp.int32 else pltpu.VMEM for item in operands]
    return pl.pallas_call(
        kernel,
        in_specs=[pl.BlockSpec(memory_space=space) for space in spaces],
        out_shape=jax.ShapeDtypeStruct((blocks, t, size), HALF),
        scratch_shapes=[pltpu.VMEM((blocks * size, width), HALF), *scratch],
    )(*operands)


def local(factor_panel, right_side, block_inverse):
    x = lax.axis_index("x")
    z = lax.axis_index("z")
    core = lax.axis_index("core")
    blk = lax.axis_index("blk")
    row = (x * NZ + z) * NC + core
    n_blk = right_side.shape[1] // factor_panel.shape[2]
    pixels, _, width = factor_panel.shape
    dates_local = right_side.shape[0]
    dates_x = dates_local // NX
    t = dates_x * n_blk
    rows_local = block_inverse.shape[1]
    per_blk = width // rows_local
    half = width // NC

    pivot = right_side.astype(HALF).reshape(NX, dates_x, pixels)
    mine = jnp.where(x == 0, pivot[0], jnp.zeros_like(pivot[0]))
    for k in range(1, NX):
        mine = mine + lax.ppermute(pivot[k], ("x", "z"), [(0, k * NZ)])

    inverse = gather_by_swap(block_inverse.astype(HALF), "x", NX)
    pivot = swap_blocks(mine.reshape(dates_x, n_blk, width).transpose(1, 0, 2), "blk")
    pivot = lax.all_gather(pivot.reshape(t, width), "core", axis=0, tiled=False)

    panels = factor_panel.transpose(1, 0, 2)
    halves = panels[0].reshape(n_blk, NC, half, width)
    sent = lax.ppermute(halves[:, 0], ("x", "z", "core"), [(1, 0)])
    lower = jnp.where(core == 1, halves[:, 1], sent)
    owner = ((x == 0) & (z == 0)).astype(jnp.int32).reshape(1)
    cross = [lower] + [lax.ppermute(lower, ("x", "z"), [(0, k * NZ)]) for k in range(1, NX)]

    place = jnp.arange(width)
    c_of, q_of, i_of = place // half, place % half // rows_local, place % rows_local
    natural = (q_of * NC + c_of) * rows_local + i_of
    order = (natural[:, None] == place[None, :]).astype(HALF)
    pair_order = order.reshape(NC, half, width).transpose(0, 2, 1)
    sizes = (n_blk, t, half, width)


    def ordered(value):
        return jnp.dot(value, order, preferred_element_type=WIDE).astype(HALF)

    def both_cores(value):
        pair = lax.all_gather(value, "core", axis=0, tiled=False)
        return jnp.concatenate([pair[0], pair[1]], axis=-1)

    extra = 128
    pick = jnp.arange(extra)
    at = pick // rows_local * width + row % per_blk * rows_local + pick % rows_local
    wanted = (pick < STEPS * rows_local) & (row // per_blk == blk)
    select = wanted[:, None] & (at[:, None] == jnp.arange(STEPS * width)[None, :])
    select = select.astype(HALF)
    pivot, pair_order, order, select = lax.optimization_barrier((pivot, pair_order, order, select))

    planes = [inverse] + [lax.ppermute(inverse, "z", [(k, 0)]) for k in range(1, NZ)]
    partial = run_kernel(first_kernel, *sizes, (), pivot[0], *planes)
    first = scatter_sum(partial).astype(HALF)
    first, panels = lax.optimization_barrier((first, panels))
    pair = lax.all_gather(first, "core", axis=0, tiled=False)
    partial = run_kernel(cross_kernel, *sizes, (), owner, pair, pair_order, *cross)
    update = scatter_sum(partial)
    pair = lax.all_gather(update, "core", axis=0, tiled=False)
    scratch = (pltpu.VMEM((t, width), HALF),)
    partial = run_kernel(second_kernel, *sizes, scratch, pivot[1], pair, *planes)
    second = scatter_sum(partial).astype(HALF)

    solved = jnp.stack([first, second])
    spread = jnp.where(z == 0, solved, jnp.zeros_like(solved))
    for k in range(1, NZ):
        spread = spread + lax.ppermute(solved, "z", [(0, k)])
    spread = ordered(both_cores(gather_by_swap(spread, "x", NX)))
    spread = spread.reshape(NX, STEPS, n_blk, dates_x, width).transpose(2, 0, 3, 1, 4)
    spread = spread.reshape(dates_local * n_blk, STEPS * width)

    panel = jnp.concatenate(
        [
            jnp.where(row > k, panels[k], jnp.zeros((), HALF))
            for k in range(STEPS)
        ],
        axis=1,
    )
    panel = jnp.concatenate([panel, select], axis=0)

    total = product(spread, panel).astype(HALF)
    lanes, rows8 = 128, 8
    total = total.reshape(n_blk * dates_local // rows8, rows8, -1, lanes).transpose(0, 2, 1, 3)
    total = swap_blocks(total.reshape(n_blk, -1, lanes), "blk")
    total = jnp.sum(total.astype(WIDE), axis=0)
    total = total.reshape(dates_local // rows8, -1, rows8, lanes).transpose(0, 2, 1, 3)
    total = total.reshape(dates_local, pixels + extra)
    answer = total[:, pixels : pixels + STEPS * rows_local]
    answer = answer.reshape(dates_local, STEPS, rows_local).transpose(1, 0, 2)
    return (answer, right_side - total[:, :pixels])


def solution(mesh):
    shape = (NX, NZ, NC, mesh.shape["blk"])
    fine = Mesh(mesh.devices.reshape(shape), ("x", "z", "core", "blk"))
    row = ("x", "z", "core")
    return jax.shard_map(
        local,
        mesh=fine,
        in_specs=(P(row, None, "blk"), P("blk", row), P(None, row, "blk")),
        out_specs=(P(None, "blk", row), P("blk", row)),
        check_vma=False,
    )
```

```python
import jax
import jax.numpy as jnp
from jax import lax
from jax.experimental import pallas as pl
from jax.experimental.pallas import tpu as pltpu
from jax.sharding import Mesh, PartitionSpec as P


STEPS = 2
NX, NZ, NC = 4, 8, 2
HALF = jnp.bfloat16
WIDE = jnp.float32


def swap_blocks(array, axis):
    return lax.all_to_all(array, axis, split_axis=0, concat_axis=0, tiled=True)


def gather_by_swap(array, axis, count):
    return swap_blocks(jnp.broadcast_to(array[None], (count, *array.shape)), axis)


def product(left, right):
    return lax.dot_general(left, right, (((1,), (1,)), ((), ())), preferred_element_type=WIDE)


def scatter_sum(split):
    return jnp.sum(swap_blocks(split, "blk").astype(WIDE), axis=0)


def assemble(planes, step, whole):
    for z, plane in enumerate(planes):
        count, _, size, _ = plane.shape
        for x in range(count):
            at = (x * len(planes) + z) * size
            whole[at : at + size, :] = plane[x, step]


def write_blocks(value, whole, out):
    size = out.shape[2]
    total = product(value, whole[...]).astype(out.dtype)
    for g in range(out.shape[0]):
        out[g] = total[:, g * size : (g + 1) * size]


def first_kernel(pivot, *refs):
    planes, (out, whole) = refs[:NZ], refs[NZ:]
    assemble(planes, 0, whole)
    write_blocks(pivot[...], whole, out)


def cross_kernel(owner, pair, order, own, *refs):
    others, (out, whole) = refs[: NX - 1], refs[NX - 1 :]
    value = product(pair[0], order[0])
    for c in range(1, NC):
        value = value + product(pair[c], order[c])
    blocks, size, _ = own.shape

    @pl.when(owner[0] == 1)
    def _():
        for g in range(blocks):
            whole[g * size : (g + 1) * size, :] = own[g]

    @pl.when(owner[0] == 0)
    def _():
        for g in range(blocks):
            part = others[0][g]
            for other in others[1:]:
                part = part + other[g]
            whole[g * size : (g + 1) * size, :] = part

    write_blocks(value.astype(HALF), whole, out)


def second_kernel(pivot, update, *refs):
    planes, (out, whole, value) = refs[:NZ], refs[NZ:]
    assemble(planes, 1, whole)
    half = update.shape[2]
    for c in range(NC):
        part = pivot[:, c * half : (c + 1) * half].astype(WIDE) - update[c]
        value[:, c * half : (c + 1) * half] = part.astype(HALF)
    write_blocks(value[...], whole, out)


def run_kernel(kernel, blocks, t, size, width, scratch, *operands):
    spaces = [pltpu.SMEM if item.dtype == jnp.int32 else pltpu.VMEM for item in operands]
    return pl.pallas_call(
        kernel,
        in_specs=[pl.BlockSpec(memory_space=space) for space in spaces],
        out_shape=jax.ShapeDtypeStruct((blocks, t, size), HALF),
        scratch_shapes=[pltpu.VMEM((blocks * size, width), HALF), *scratch],
    )(*operands)


def local(factor_panel, right_side, block_inverse):
    x = lax.axis_index("x")
    z = lax.axis_index("z")
    core = lax.axis_index("core")
    blk = lax.axis_index("blk")
    row = (x * NZ + z) * NC + core
    n_blk = right_side.shape[1] // factor_panel.shape[2]
    pixels, _, width = factor_panel.shape
    dates_local = right_side.shape[0]
    dates_x = dates_local // NX
    t = dates_x * n_blk
    rows_local = block_inverse.shape[1]
    per_blk = width // rows_local
    half = width // NC

    copies = block_inverse.astype(HALF).reshape(1, STEPS * rows_local, width)
    copies = jnp.broadcast_to(copies, (NX, *copies.shape[1:]))
    pivot = right_side.astype(HALF).reshape(NX, dates_x, n_blk, width)
    pivot = pivot.transpose(0, 2, 1, 3).reshape(NX, n_blk * dates_x, width)
    both = swap_blocks(jnp.concatenate([copies, pivot], axis=1), "x")
    inverse = both[:, : STEPS * rows_local].reshape(NX, STEPS, rows_local, width)
    mine = both[0, STEPS * rows_local :].reshape(n_blk, dates_x, width)

    pivot = swap_blocks(mine, "blk")
    pivot = lax.all_gather(pivot.reshape(t, width), "core", axis=0, tiled=False)

    panels = factor_panel.transpose(1, 0, 2)
    halves = panels[0].reshape(n_blk, NC, half, width)
    sent = lax.ppermute(halves[:, 0], ("x", "z", "core"), [(1, 0)])
    lower = jnp.where(core == 1, halves[:, 1], sent)
    owner = ((x == 0) & (z == 0)).astype(jnp.int32).reshape(1)
    cross = [lower] + [lax.ppermute(lower, ("x", "z"), [(0, k * NZ)]) for k in range(1, NX)]

    place = jnp.arange(width)
    c_of, q_of, i_of = place // half, place % half // rows_local, place % rows_local
    natural = (q_of * NC + c_of) * rows_local + i_of
    order = (natural[:, None] == place[None, :]).astype(HALF)
    pair_order = order.reshape(NC, half, width).transpose(0, 2, 1)
    sizes = (n_blk, t, half, width)


    def ordered(value):
        return jnp.dot(value, order, preferred_element_type=WIDE).astype(HALF)

    def both_cores(value):
        pair = lax.all_gather(value, "core", axis=0, tiled=False)
        return jnp.concatenate([pair[0], pair[1]], axis=-1)

    extra = 128
    pick = jnp.arange(extra)
    at = pick // rows_local * width + row % per_blk * rows_local + pick % rows_local
    wanted = (pick < STEPS * rows_local) & (row // per_blk == blk)
    select = wanted[:, None] & (at[:, None] == jnp.arange(STEPS * width)[None, :])
    select = select.astype(HALF)

    planes = [inverse] + [lax.ppermute(inverse, "z", [(k, 0)]) for k in range(1, NZ)]
    partial = run_kernel(first_kernel, *sizes, (), pivot[0], *planes)
    first = scatter_sum(partial).astype(HALF)
    first, panels = lax.optimization_barrier((first, panels))
    pair = lax.all_gather(first, "core", axis=0, tiled=False)
    partial = run_kernel(cross_kernel, *sizes, (), owner, pair, pair_order, *cross)
    update = scatter_sum(partial)
    pair = lax.all_gather(update, "core", axis=0, tiled=False)
    scratch = (pltpu.VMEM((t, width), HALF),)
    partial = run_kernel(second_kernel, *sizes, scratch, pivot[1], pair, *planes)
    second = scatter_sum(partial).astype(HALF)

    solved = jnp.stack([first, second])
    spread = jnp.where(z == 0, solved, jnp.zeros_like(solved))
    for k in range(1, NZ):
        spread = spread + lax.ppermute(solved, "z", [(0, k)])
    spread = ordered(both_cores(gather_by_swap(spread, "x", NX)))
    spread = spread.reshape(NX, STEPS, n_blk, dates_x, width).transpose(2, 0, 3, 1, 4)
    spread = spread.reshape(dates_local * n_blk, STEPS * width)

    panel = jnp.concatenate(
        [
            jnp.where(row > k, panels[k], jnp.zeros((), HALF))
            for k in range(STEPS)
        ],
        axis=1,
    )
    panel = jnp.concatenate([panel, select], axis=0)

    total = product(spread, panel).astype(HALF)
    lanes, rows8 = 128, 8
    total = total.reshape(n_blk * dates_local // rows8, rows8, -1, lanes).transpose(0, 2, 1, 3)
    total = swap_blocks(total.reshape(n_blk, -1, lanes), "blk")
    total = jnp.sum(total.astype(WIDE), axis=0)
    total = total.reshape(dates_local // rows8, -1, rows8, lanes).transpose(0, 2, 1, 3)
    total = total.reshape(dates_local, pixels + extra)
    answer = total[:, pixels : pixels + STEPS * rows_local]
    answer = answer.reshape(dates_local, STEPS, rows_local).transpose(1, 0, 2)
    return (answer, right_side - total[:, :pixels])


def solution(mesh):
    shape = (NX, NZ, NC, mesh.shape["blk"])
    fine = Mesh(mesh.devices.reshape(shape), ("x", "z", "core", "blk"))
    row = ("x", "z", "core")
    return jax.shard_map(
        local,
        mesh=fine,
        in_specs=(P(row, None, "blk"), P("blk", row), P(None, row, "blk")),
        out_specs=(P(None, "blk", row), P("blk", row)),
        check_vma=False,
    )
```

```python
import jax
import jax.numpy as jnp
from jax import lax
from jax.experimental import pallas as pl
from jax.experimental.pallas import tpu as pltpu
from jax.sharding import Mesh, PartitionSpec as P


STEPS = 2
NX, NZ, NC = 4, 8, 2
HALF = jnp.bfloat16
WIDE = jnp.float32


def swap_blocks(array, axis):
    return lax.all_to_all(array, axis, split_axis=0, concat_axis=0, tiled=True)


def gather_by_swap(array, axis, count):
    return swap_blocks(jnp.broadcast_to(array[None], (count, *array.shape)), axis)


def product(left, right):
    return lax.dot_general(left, right, (((1,), (1,)), ((), ())), preferred_element_type=WIDE)


def scatter_sum(split):
    return jnp.sum(swap_blocks(split, "blk").astype(WIDE), axis=0)


def assemble(planes, step, whole, done):
    copies = []
    for z, plane in enumerate(planes):
        count, _, size, _ = plane.shape
        for x in range(count):
            at = (x * len(planes) + z) * size
            target = whole.at[at : at + size, :]
            copies.append(pltpu.make_async_copy(plane.at[x, step], target, done.at[len(copies)]))
    for copy in copies:
        copy.start()
    return copies


def write_blocks(value, whole, out):
    size = out.shape[2]
    total = product(value, whole[...]).astype(out.dtype)
    for g in range(out.shape[0]):
        out[g] = total[:, g * size : (g + 1) * size]


def first_kernel(pivot, *refs):
    planes, (out, whole, done) = refs[:NZ], refs[NZ:]
    for copy in assemble(planes, 0, whole, done):
        copy.wait()
    write_blocks(pivot[...], whole, out)


def cross_kernel(which, pair, order, *refs):
    panels, (out, whole, done) = refs[:NX], refs[NX:]
    for k in range(NX):

        @pl.when(which[0] == k)
        def _():
            copy = pltpu.make_async_copy(panels[k], whole, done.at[0])
            copy.start()
            copy.wait()

    value = product(pair[0], order[0])
    for c in range(1, NC):
        value = value + product(pair[c], order[c])
    write_blocks(value.astype(HALF), whole, out)


def second_kernel(pivot, update, *refs):
    planes, (out, whole, done, value) = refs[:NZ], refs[NZ:]
    copies = assemble(planes, 1, whole, done)
    half = update.shape[2]
    for c in range(NC):
        part = pivot[:, c * half : (c + 1) * half].astype(WIDE) - update[c]
        value[:, c * half : (c + 1) * half] = part.astype(HALF)
    for copy in copies:
        copy.wait()
    write_blocks(value[...], whole, out)


def run_kernel(kernel, blocks, t, size, width, scratch, near, far):
    spaces = [pltpu.SMEM if item.dtype == jnp.int32 else pltpu.VMEM for item in near]
    spaces += [pl.ANY] * len(far)
    whole = pltpu.VMEM((blocks * size, width), HALF)
    done = pltpu.SemaphoreType.DMA((NX * NZ,))
    return pl.pallas_call(
        kernel,
        in_specs=[pl.BlockSpec(memory_space=space) for space in spaces],
        out_shape=jax.ShapeDtypeStruct((blocks, t, size), HALF),
        scratch_shapes=[whole, done, *scratch],
    )(*near, *far)


def local(factor_panel, right_side, block_inverse):
    x = lax.axis_index("x")
    z = lax.axis_index("z")
    core = lax.axis_index("core")
    blk = lax.axis_index("blk")
    row = (x * NZ + z) * NC + core
    n_blk = right_side.shape[1] // factor_panel.shape[2]
    pixels, _, width = factor_panel.shape
    dates_local = right_side.shape[0]
    dates_x = dates_local // NX
    t = dates_x * n_blk
    rows_local = block_inverse.shape[1]
    per_blk = width // rows_local
    half = width // NC

    copies = block_inverse.astype(HALF).reshape(1, STEPS * rows_local, width)
    copies = jnp.broadcast_to(copies, (NX, *copies.shape[1:]))
    pivot = right_side.astype(HALF).reshape(NX, dates_x, n_blk, width)
    pivot = pivot.transpose(0, 2, 1, 3).reshape(NX, n_blk * dates_x, width)
    both = swap_blocks(jnp.concatenate([copies, pivot], axis=1), "x")
    inverse = both[:, : STEPS * rows_local].reshape(NX, STEPS, rows_local, width)
    mine = both[0, STEPS * rows_local :].reshape(n_blk, dates_x, width)

    pivot = swap_blocks(mine, "blk")
    pivot = lax.all_gather(pivot.reshape(t, width), "core", axis=0, tiled=False)

    panels = factor_panel.transpose(1, 0, 2)
    halves = panels[0].reshape(n_blk, NC, half, width)
    sent = lax.ppermute(halves[:, 0], ("x", "z", "core"), [(1, 0)])
    lower = jnp.where(core == 1, halves[:, 1], sent)
    which = x.astype(jnp.int32).reshape(1)
    flat = lower.reshape(n_blk * half, width)
    cross = [flat] + [lax.ppermute(flat, ("x", "z"), [(0, k * NZ)]) for k in range(1, NX)]

    place = jnp.arange(width)
    c_of, q_of, i_of = place // half, place % half // rows_local, place % rows_local
    natural = (q_of * NC + c_of) * rows_local + i_of
    order = (natural[:, None] == place[None, :]).astype(HALF)
    pair_order = order.reshape(NC, half, width).transpose(0, 2, 1)
    sizes = (n_blk, t, half, width)


    def ordered(value):
        return jnp.dot(value, order, preferred_element_type=WIDE).astype(HALF)

    def both_cores(value):
        pair = lax.all_gather(value, "core", axis=0, tiled=False)
        return jnp.concatenate([pair[0], pair[1]], axis=-1)

    extra = 128
    pick = jnp.arange(extra)
    at = pick // rows_local * width + row % per_blk * rows_local + pick % rows_local
    wanted = (pick < STEPS * rows_local) & (row // per_blk == blk)
    select = wanted[:, None] & (at[:, None] == jnp.arange(STEPS * width)[None, :])
    select = select.astype(HALF)

    planes = [inverse] + [lax.ppermute(inverse, "z", [(k, 0)]) for k in range(1, NZ)]
    partial = run_kernel(first_kernel, *sizes, (), (pivot[0],), planes)
    first = scatter_sum(partial).astype(HALF)
    first, panels = lax.optimization_barrier((first, panels))
    pair = lax.all_gather(first, "core", axis=0, tiled=False)
    partial = run_kernel(cross_kernel, *sizes, (), (which, pair, pair_order), cross)
    update = scatter_sum(partial)
    pair = lax.all_gather(update, "core", axis=0, tiled=False)
    scratch = (pltpu.VMEM((t, width), HALF),)
    partial = run_kernel(second_kernel, *sizes, scratch, (pivot[1], pair), planes)
    second = scatter_sum(partial).astype(HALF)

    solved = jnp.stack([first, second])
    spread = jnp.where(z == 0, solved, jnp.zeros_like(solved))
    for k in range(1, NZ):
        received = lax.ppermute(solved, "z", [(0, k)])
        spread = spread + received
    spread = ordered(both_cores(gather_by_swap(spread, "x", NX)))
    spread = spread.reshape(NX, STEPS, n_blk, dates_x, width).transpose(2, 0, 3, 1, 4)
    spread = spread.reshape(dates_local * n_blk, STEPS * width)

    panel = jnp.concatenate(
        [
            jnp.where(row > k, panels[k], jnp.zeros((), HALF))
            for k in range(STEPS)
        ],
        axis=1,
    )
    panel = jnp.concatenate([panel, select], axis=0)

    total = product(spread, panel).astype(HALF)
    lanes, rows8 = 128, 8
    total = total.reshape(n_blk * dates_local // rows8, rows8, -1, lanes).transpose(0, 2, 1, 3)
    total = swap_blocks(total.reshape(n_blk, -1, lanes), "blk")
    total = jnp.sum(total.astype(WIDE), axis=0)
    total = total.reshape(dates_local // rows8, -1, rows8, lanes).transpose(0, 2, 1, 3)
    total = total.reshape(dates_local, pixels + extra)
    answer = total[:, pixels : pixels + STEPS * rows_local]
    answer = answer.reshape(dates_local, STEPS, rows_local).transpose(1, 0, 2)
    return (answer, right_side - total[:, :pixels])


def solution(mesh):
    shape = (NX, NZ, NC, mesh.shape["blk"])
    fine = Mesh(mesh.devices.reshape(shape), ("x", "z", "core", "blk"))
    row = ("x", "z", "core")
    return jax.shard_map(
        local,
        mesh=fine,
        in_specs=(P(row, None, "blk"), P("blk", row), P(None, row, "blk")),
        out_specs=(P(None, "blk", row), P("blk", row)),
        check_vma=False,
    )
```

```python
import jax
import jax.numpy as jnp
from jax import lax
from jax.experimental import pallas as pl
from jax.experimental.pallas import tpu as pltpu
from jax.sharding import Mesh, PartitionSpec as P


STEPS = 2
NX, NZ, NC = 4, 8, 2
HALF = jnp.bfloat16
WIDE = jnp.float32


def swap_blocks(array, axis):
    return lax.all_to_all(array, axis, split_axis=0, concat_axis=0, tiled=True)


def gather_by_swap(array, axis, count):
    return swap_blocks(jnp.broadcast_to(array[None], (count, *array.shape)), axis)


def product(left, right):
    return lax.dot_general(left, right, (((1,), (1,)), ((), ())), preferred_element_type=WIDE)


def scatter_sum(split):
    return jnp.sum(swap_blocks(split, "blk").astype(WIDE), axis=0)


def assemble(planes, step, whole):
    for z, plane in enumerate(planes):
        count, _, size, _ = plane.shape
        for x in range(count):
            at = (x * len(planes) + z) * size
            whole[at : at + size, :] = plane[x, step]


def write_blocks(value, whole, out):
    size = out.shape[2]
    total = product(value, whole[...]).astype(out.dtype)
    for g in range(out.shape[0]):
        out[g] = total[:, g * size : (g + 1) * size]


def first_kernel(pivot, *refs):
    planes, (out, whole) = refs[:NZ], refs[NZ:]
    assemble(planes, 0, whole)
    write_blocks(pivot[...], whole, out)


def cross_kernel(owner, pair, order, own, *refs):
    others, (out, whole) = refs[: NX - 1], refs[NX - 1 :]
    value = product(pair[0], order[0])
    for c in range(1, NC):
        value = value + product(pair[c], order[c])
    blocks, size, _ = own.shape

    @pl.when(owner[0] == 1)
    def _():
        for g in range(blocks):
            whole[g * size : (g + 1) * size, :] = own[g]

    @pl.when(owner[0] == 0)
    def _():
        for g in range(blocks):
            part = others[0][g]
            for other in others[1:]:
                part = part + other[g]
            whole[g * size : (g + 1) * size, :] = part

    write_blocks(value.astype(HALF), whole, out)


def second_kernel(pivot, update, *refs):
    planes, (out, whole, value) = refs[:NZ], refs[NZ:]
    assemble(planes, 1, whole)
    half = update.shape[2]
    for c in range(NC):
        part = pivot[:, c * half : (c + 1) * half].astype(WIDE) - update[c]
        value[:, c * half : (c + 1) * half] = part.astype(HALF)
    write_blocks(value[...], whole, out)


def run_kernel(kernel, blocks, t, size, width, scratch, *operands):
    spaces = [pltpu.SMEM if item.dtype == jnp.int32 else pltpu.VMEM for item in operands]
    return pl.pallas_call(
        kernel,
        in_specs=[pl.BlockSpec(memory_space=space) for space in spaces],
        out_shape=jax.ShapeDtypeStruct((blocks, t, size), HALF),
        scratch_shapes=[pltpu.VMEM((blocks * size, width), HALF), *scratch],
    )(*operands)


def local(factor_panel, right_side, block_inverse):
    x = lax.axis_index("x")
    z = lax.axis_index("z")
    core = lax.axis_index("core")
    blk = lax.axis_index("blk")
    row = (x * NZ + z) * NC + core
    n_blk = right_side.shape[1] // factor_panel.shape[2]
    pixels, _, width = factor_panel.shape
    dates_local = right_side.shape[0]
    dates_x = dates_local // NX
    t = dates_x * n_blk
    rows_local = block_inverse.shape[1]
    per_blk = width // rows_local
    half = width // NC

    copies = block_inverse.astype(HALF).reshape(1, STEPS * rows_local, width)
    copies = jnp.broadcast_to(copies, (NX, *copies.shape[1:]))
    pivot = right_side.astype(HALF).reshape(NX, dates_x, n_blk, width)
    pivot = pivot.transpose(0, 2, 1, 3).reshape(NX, n_blk * dates_x, width)
    both = swap_blocks(jnp.concatenate([copies, pivot], axis=1), "x")
    inverse = both[:, : STEPS * rows_local].reshape(NX, STEPS, rows_local, width)
    mine = both[0, STEPS * rows_local :].reshape(n_blk, dates_x, width)

    pivot = swap_blocks(mine, "blk")
    pivot = lax.all_gather(pivot.reshape(t, width), "core", axis=0, tiled=False)

    panels = factor_panel.transpose(1, 0, 2)
    halves = panels[0].reshape(n_blk, NC, half, width)
    sent = lax.ppermute(halves[:, 0], ("x", "z", "core"), [(1, 0)])
    lower = jnp.where(core == 1, halves[:, 1], sent)
    owner = ((x == 0) & (z == 0)).astype(jnp.int32).reshape(1)
    cross = [lower] + [lax.ppermute(lower, ("x", "z"), [(0, k * NZ)]) for k in range(1, NX)]

    place = jnp.arange(width)
    c_of, q_of, i_of = place // half, place % half // rows_local, place % rows_local
    natural = (q_of * NC + c_of) * rows_local + i_of
    order = (natural[:, None] == place[None, :]).astype(HALF)
    pair_order = order.reshape(NC, half, width).transpose(0, 2, 1)
    sizes = (n_blk, t, half, width)


    def ordered(value):
        return jnp.dot(value, order, preferred_element_type=WIDE).astype(HALF)

    def both_cores(value):
        pair = lax.all_gather(value, "core", axis=0, tiled=False)
        return jnp.concatenate([pair[0], pair[1]], axis=-1)

    extra = 128
    pick = jnp.arange(extra)
    at = pick // rows_local * width + row % per_blk * rows_local + pick % rows_local
    wanted = (pick < STEPS * rows_local) & (row // per_blk == blk)
    select = wanted[:, None] & (at[:, None] == jnp.arange(STEPS * width)[None, :])
    select = select.astype(HALF)

    planes = [inverse] + [lax.ppermute(inverse, "z", [(k, 0)]) for k in range(1, NZ)]

    def first_half(pivot, planes):
        partial = run_kernel(first_kernel, *sizes, (), pivot, *planes)
        first = scatter_sum(partial).astype(HALF)
        return first, lax.all_gather(first, "core", axis=0, tiled=False)

    def second_half(first, pair, pivot, planes, cross):
        partial = run_kernel(cross_kernel, *sizes, (), owner, pair, pair_order, *cross)
        pair = lax.all_gather(scatter_sum(partial), "core", axis=0, tiled=False)
        scratch = (pltpu.VMEM((t, width), HALF),)
        partial = run_kernel(second_kernel, *sizes, scratch, pivot, pair, *planes)
        return jnp.stack([first, scatter_sum(partial).astype(HALF)])

    def none_first(pivot, planes):
        return jnp.zeros((t, half), HALF), jnp.zeros((NC, t, half), HALF)

    def none_second(first, pair, pivot, planes, cross):
        return jnp.zeros((STEPS, t, half), HALF)

    first, pair = lax.cond(z == 0, first_half, none_first, pivot[0], planes)
    first, panels = lax.optimization_barrier((first, panels))
    solved = lax.cond(
        z == 0, second_half, none_second, first, pair, pivot[1], planes, cross
    )

    spread = solved
    for k in range(1, NZ):
        received = lax.ppermute(solved, "z", [(0, k)])
        spread = spread + received
    spread = ordered(both_cores(gather_by_swap(spread, "x", NX)))
    spread = spread.reshape(NX, STEPS, n_blk, dates_x, width).transpose(2, 0, 3, 1, 4)
    spread = spread.reshape(dates_local * n_blk, STEPS * width)

    panel = jnp.concatenate(
        [
            jnp.where(row > k, panels[k], jnp.zeros((), HALF))
            for k in range(STEPS)
        ],
        axis=1,
    )
    panel = jnp.concatenate([panel, select], axis=0)

    total = product(spread, panel).astype(HALF)
    lanes, rows8 = 128, 8
    total = total.reshape(n_blk * dates_local // rows8, rows8, -1, lanes).transpose(0, 2, 1, 3)
    total = swap_blocks(total.reshape(n_blk, -1, lanes), "blk")
    total = jnp.sum(total.astype(WIDE), axis=0)
    total = total.reshape(dates_local // rows8, -1, rows8, lanes).transpose(0, 2, 1, 3)
    total = total.reshape(dates_local, pixels + extra)
    answer = total[:, pixels : pixels + STEPS * rows_local]
    answer = answer.reshape(dates_local, STEPS, rows_local).transpose(1, 0, 2)
    return (answer, right_side - total[:, :pixels])


def solution(mesh):
    shape = (NX, NZ, NC, mesh.shape["blk"])
    fine = Mesh(mesh.devices.reshape(shape), ("x", "z", "core", "blk"))
    row = ("x", "z", "core")
    return jax.shard_map(
        local,
        mesh=fine,
        in_specs=(P(row, None, "blk"), P("blk", row), P(None, row, "blk")),
        out_specs=(P(None, "blk", row), P("blk", row)),
        check_vma=False,
    )
```

```python
import jax
import jax.numpy as jnp
from jax import lax
from jax.experimental import pallas as pl
from jax.experimental.pallas import tpu as pltpu
from jax.sharding import Mesh, PartitionSpec as P


STEPS = 2
NX, NZ, NC = 4, 8, 2
HALF = jnp.bfloat16
WIDE = jnp.float32


def swap_blocks(array, axis):
    return lax.all_to_all(array, axis, split_axis=0, concat_axis=0, tiled=True)


def gather_by_swap(array, axis, count):
    return swap_blocks(jnp.broadcast_to(array[None], (count, *array.shape)), axis)


def product(left, right):
    return lax.dot_general(left, right, (((1,), (1,)), ((), ())), preferred_element_type=WIDE)


def scatter_sum(split):
    return jnp.sum(swap_blocks(split, "blk").astype(WIDE), axis=0)


def assemble(planes, step, whole):
    for z, plane in enumerate(planes):
        count, _, size, _ = plane.shape
        for x in range(count):
            at = (x * len(planes) + z) * size
            whole[at : at + size, :] = plane[x, step]


def write_blocks(value, whole, out):
    size = out.shape[2]
    total = product(value, whole[...]).astype(out.dtype)
    for g in range(out.shape[0]):
        out[g] = total[:, g * size : (g + 1) * size]


def pack_kernel(inverse, pivot, out):
    count, _, width = out.shape
    steps, size, _ = inverse.shape
    dates = pivot.shape[0] // count
    for x in range(count):
        for k in range(steps):
            out[x, k * size : (k + 1) * size, :] = inverse[k].astype(out.dtype)
        for g in range(pivot.shape[1] // width):
            at = steps * size + g * dates
            part = pivot[x * dates : (x + 1) * dates, g * width : (g + 1) * width]
            out[x, at : at + dates, :] = part.astype(out.dtype)


def first_kernel(pivot, *refs):
    planes, (out, whole) = refs[:NZ], refs[NZ:]
    assemble(planes, 0, whole)
    write_blocks(pivot[0], whole, out)


def cross_kernel(owner, pair, order, own, *refs):
    others, (out, whole) = refs[: NX - 1], refs[NX - 1 :]
    value = product(pair[0], order[0])
    for c in range(1, NC):
        value = value + product(pair[c], order[c])
    blocks, size, _ = own.shape

    @pl.when(owner[0] == 1)
    def _():
        for g in range(blocks):
            whole[g * size : (g + 1) * size, :] = own[g]

    @pl.when(owner[0] == 0)
    def _():
        for g in range(blocks):
            part = others[0][g]
            for other in others[1:]:
                part = part + other[g]
            whole[g * size : (g + 1) * size, :] = part

    write_blocks(value.astype(HALF), whole, out)


def second_kernel(pivot, update, *refs):
    planes, (out, whole, value) = refs[:NZ], refs[NZ:]
    assemble(planes, 1, whole)
    half = update.shape[2]
    for c in range(NC):
        part = pivot[1, :, c * half : (c + 1) * half].astype(WIDE) - update[c]
        value[:, c * half : (c + 1) * half] = part.astype(HALF)
    write_blocks(value[...], whole, out)


def run_kernel(kernel, blocks, t, size, width, scratch, *operands):
    spaces = [pltpu.SMEM if item.dtype == jnp.int32 else pltpu.VMEM for item in operands]
    return pl.pallas_call(
        kernel,
        in_specs=[pl.BlockSpec(memory_space=space) for space in spaces],
        out_shape=jax.ShapeDtypeStruct((blocks, t, size), HALF),
        scratch_shapes=[pltpu.VMEM((blocks * size, width), HALF), *scratch],
    )(*operands)


def local(factor_panel, right_side, block_inverse):
    x = lax.axis_index("x")
    z = lax.axis_index("z")
    core = lax.axis_index("core")
    blk = lax.axis_index("blk")
    row = (x * NZ + z) * NC + core
    n_blk = right_side.shape[1] // factor_panel.shape[2]
    pixels, _, width = factor_panel.shape
    dates_local = right_side.shape[0]
    dates_x = dates_local // NX
    t = dates_x * n_blk
    rows_local = block_inverse.shape[1]
    per_blk = width // rows_local
    half = width // NC

    packed = pl.pallas_call(
        pack_kernel,
        out_shape=jax.ShapeDtypeStruct(
            (NX, STEPS * rows_local + n_blk * dates_x, width), HALF
        ),
    )(block_inverse, right_side)
    both = swap_blocks(packed, "x")
    inverse = both[:, : STEPS * rows_local].reshape(NX, STEPS, rows_local, width)
    mine = both[0, STEPS * rows_local :].reshape(n_blk, dates_x, width)

    pivot = swap_blocks(mine, "blk")
    pivot = lax.all_gather(pivot.reshape(t, width), "core", axis=0, tiled=False)

    panels = factor_panel.transpose(1, 0, 2)
    halves = panels[0].reshape(n_blk, NC, half, width)
    sent = lax.ppermute(halves[:, 0], ("x", "z", "core"), [(1, 0)])
    lower = jnp.where(core == 1, halves[:, 1], sent)
    owner = ((x == 0) & (z == 0)).astype(jnp.int32).reshape(1)
    cross = [lower] + [lax.ppermute(lower, ("x", "z"), [(0, k * NZ)]) for k in range(1, NX)]

    place = jnp.arange(width)
    c_of, q_of, i_of = place // half, place % half // rows_local, place % rows_local
    natural = (q_of * NC + c_of) * rows_local + i_of
    order = (natural[:, None] == place[None, :]).astype(HALF)
    pair_order = order.reshape(NC, half, width).transpose(0, 2, 1)
    sizes = (n_blk, t, half, width)


    def ordered(value):
        return jnp.dot(value, order, preferred_element_type=WIDE).astype(HALF)

    def both_cores(value):
        pair = lax.all_gather(value, "core", axis=0, tiled=False)
        return jnp.concatenate([pair[0], pair[1]], axis=-1)

    planes = [inverse]
    for k in range(1, NZ):
        planes.append(lax.ppermute(inverse, "z", [(k, 0)]))

    def first_half(pivot, planes):
        partial = run_kernel(first_kernel, *sizes, (), pivot, *planes)
        first = scatter_sum(partial).astype(HALF)
        return first, lax.all_gather(first, "core", axis=0, tiled=False)

    def second_half(first, pair, pivot, planes, cross):
        partial = run_kernel(cross_kernel, *sizes, (), owner, pair, pair_order, *cross)
        pair = lax.all_gather(scatter_sum(partial), "core", axis=0, tiled=False)
        scratch = (pltpu.VMEM((t, width), HALF),)
        partial = run_kernel(second_kernel, *sizes, scratch, pivot, pair, *planes)
        return jnp.stack([first, scatter_sum(partial).astype(HALF)])

    def none_first(pivot, planes):
        return jnp.zeros((t, half), HALF), jnp.zeros((NC, t, half), HALF)

    def none_second(first, pair, pivot, planes, cross):
        return jnp.zeros((STEPS, t, half), HALF)

    first, pair = lax.cond(z == 0, first_half, none_first, pivot, planes)
    solved = lax.cond(
        z == 0, second_half, none_second, first, pair, pivot, planes, cross
    )

    solved, panels, row = lax.optimization_barrier((solved, panels, row))
    extra = 128
    pick = jnp.arange(extra)
    at = pick // rows_local * width + row % per_blk * rows_local + pick % rows_local
    wanted = (pick < STEPS * rows_local) & (row // per_blk == blk)
    select = wanted[:, None] & (at[:, None] == jnp.arange(STEPS * width)[None, :])
    select = select.astype(HALF)

    spread = solved
    for k in range(1, NZ):
        received = lax.ppermute(solved, "z", [(0, k)])
        spread = spread + received
    spread = ordered(both_cores(gather_by_swap(spread, "x", NX)))
    spread = spread.reshape(NX, STEPS, n_blk, dates_x, width).transpose(2, 0, 3, 1, 4)
    spread = spread.reshape(dates_local * n_blk, STEPS * width)

    panel = jnp.concatenate(
        [
            jnp.where(row > k, panels[k], jnp.zeros((), HALF))
            for k in range(STEPS)
        ],
        axis=1,
    )
    panel = jnp.concatenate([panel, select], axis=0)

    total = product(spread, panel).astype(HALF)
    lanes, rows8 = 128, 8
    total = total.reshape(n_blk * dates_local // rows8, rows8, -1, lanes).transpose(0, 2, 1, 3)
    total = swap_blocks(total.reshape(n_blk, -1, lanes), "blk")
    total = jnp.sum(total.astype(WIDE), axis=0)
    total = total.reshape(dates_local // rows8, -1, rows8, lanes).transpose(0, 2, 1, 3)
    total = total.reshape(dates_local, pixels + extra)
    answer = total[:, pixels : pixels + STEPS * rows_local]
    answer = answer.reshape(dates_local, STEPS, rows_local).transpose(1, 0, 2)
    return (answer, right_side - total[:, :pixels])


def solution(mesh):
    shape = (NX, NZ, NC, mesh.shape["blk"])
    fine = Mesh(mesh.devices.reshape(shape), ("x", "z", "core", "blk"))
    row = ("x", "z", "core")
    return jax.shard_map(
        local,
        mesh=fine,
        in_specs=(P(row, None, "blk"), P("blk", row), P(None, row, "blk")),
        out_specs=(P(None, "blk", row), P("blk", row)),
        check_vma=False,
    )
```

```python
import functools

import jax
import jax.numpy as jnp
from jax import lax
from jax.experimental import pallas as pl
from jax.experimental.pallas import tpu as pltpu
from jax.sharding import Mesh, PartitionSpec as P


STEPS = 2
NX, NZ, NC = 4, 8, 2
HALF = jnp.bfloat16
WIDE = jnp.float32


def swap_blocks(array, axis):
    return lax.all_to_all(array, axis, split_axis=0, concat_axis=0, tiled=True)


def gather_by_swap(array, axis, count):
    return swap_blocks(jnp.broadcast_to(array[None], (count, *array.shape)), axis)


def product(left, right):
    return lax.dot_general(left, right, (((1,), (1,)), ((), ())), preferred_element_type=WIDE)


def scatter_sum(split):
    return jnp.sum(swap_blocks(split, "blk").astype(WIDE), axis=0)


def assemble(planes, step, whole):
    for z, plane in enumerate(planes):
        count, _, size, _ = plane.shape
        for x in range(count):
            at = (x * len(planes) + z) * size
            whole[at : at + size, :] = plane[x, step]


def write_blocks(value, whole, out):
    size = out.shape[2]
    total = product(value, whole[...]).astype(out.dtype)
    for g in range(out.shape[0]):
        out[g] = total[:, g * size : (g + 1) * size]


def pack_kernel(inverse, pivot, out):
    count, _, width = out.shape
    steps, size, _ = inverse.shape
    dates = pivot.shape[0] // count
    for x in range(count):
        for k in range(steps):
            out[x, k * size : (k + 1) * size, :] = inverse[k].astype(out.dtype)
        for g in range(pivot.shape[1] // width):
            at = steps * size + g * dates
            part = pivot[x * dates : (x + 1) * dates, g * width : (g + 1) * width]
            out[x, at : at + dates, :] = part.astype(out.dtype)


def first_kernel(pivot, *refs):
    planes, (out, whole) = refs[:NZ], refs[NZ:]
    assemble(planes, 0, whole)
    write_blocks(pivot[0], whole, out)


def cross_kernel(rows_local, owner, pair, own, *refs):
    others, (out, whole) = refs[: NX - 1], refs[NX - 1 :]
    blocks, size, width = own.shape
    column = lax.broadcasted_iota(jnp.int32, (width, size), 0)
    place = lax.broadcasted_iota(jnp.int32, (width, size), 1)
    natural = place + place // rows_local * (rows_local * (NC - 1))
    value = jnp.zeros((pair.shape[1], width), WIDE)
    for c in range(NC):
        order = jnp.where(column == natural + c * rows_local, 1.0, 0.0).astype(HALF)
        value = value + product(pair[c], order)

    @pl.when(owner[0] == 1)
    def _():
        for g in range(blocks):
            whole[g * size : (g + 1) * size, :] = own[g]

    @pl.when(owner[0] == 0)
    def _():
        for g in range(blocks):
            part = others[0][g]
            for other in others[1:]:
                part = part + other[g]
            whole[g * size : (g + 1) * size, :] = part

    write_blocks(value.astype(HALF), whole, out)


def second_kernel(pivot, update, *refs):
    planes, (out, whole, value) = refs[:NZ], refs[NZ:]
    assemble(planes, 1, whole)
    half = update.shape[2]
    for c in range(NC):
        part = pivot[1, :, c * half : (c + 1) * half].astype(WIDE) - update[c]
        value[:, c * half : (c + 1) * half] = part.astype(HALF)
    write_blocks(value[...], whole, out)


def finish_kernel(parts, right, answer, reduced):
    lanes, rows8 = 128, 8
    pixels = right.shape[1] // lanes
    steps, dates, columns = answer.shape
    deep = parts.shape[1] * rows8 // dates
    for q in range(dates // rows8):
        at = slice(q * rows8, (q + 1) * rows8)
        total = parts[0, q * deep : (q + 1) * deep, :].astype(WIDE)
        for b in range(1, parts.shape[0]):
            total = total + parts[b, q * deep : (q + 1) * deep, :].astype(WIDE)
        for l in range(pixels):
            lane = slice(l * lanes, (l + 1) * lanes)
            reduced[at, lane] = right[at, lane] - total[l * rows8 : (l + 1) * rows8, :]
        last = total[pixels * rows8 : (pixels + 1) * rows8, :]
        for k in range(steps):
            answer[k, at, :] = last[:, k * columns : (k + 1) * columns]


def run_kernel(kernel, blocks, t, size, width, scratch, *operands):
    spaces = [pltpu.SMEM if item.dtype == jnp.int32 else pltpu.VMEM for item in operands]
    return pl.pallas_call(
        kernel,
        in_specs=[pl.BlockSpec(memory_space=space) for space in spaces],
        out_shape=jax.ShapeDtypeStruct((blocks, t, size), HALF),
        scratch_shapes=[pltpu.VMEM((blocks * size, width), HALF), *scratch],
    )(*operands)


def local(factor_panel, right_side, block_inverse):
    x = lax.axis_index("x")
    z = lax.axis_index("z")
    core = lax.axis_index("core")
    blk = lax.axis_index("blk")
    row = (x * NZ + z) * NC + core
    n_blk = right_side.shape[1] // factor_panel.shape[2]
    _, _, width = factor_panel.shape
    dates_local = right_side.shape[0]
    dates_x = dates_local // NX
    t = dates_x * n_blk
    rows_local = block_inverse.shape[1]
    per_blk = width // rows_local
    half = width // NC

    packed = pl.pallas_call(
        pack_kernel,
        out_shape=jax.ShapeDtypeStruct(
            (NX, STEPS * rows_local + n_blk * dates_x, width), HALF
        ),
    )(block_inverse, right_side)
    both = swap_blocks(packed, "x")
    inverse = both[:, : STEPS * rows_local].reshape(NX, STEPS, rows_local, width)
    mine = both[0, STEPS * rows_local :].reshape(n_blk, dates_x, width)

    pivot = swap_blocks(mine, "blk")
    pivot = lax.all_gather(pivot.reshape(t, width), "core", axis=0, tiled=False)

    panels = factor_panel.transpose(1, 0, 2)
    halves = panels[0].reshape(n_blk, NC, half, width)
    sent = lax.ppermute(halves[:, 0], ("x", "z", "core"), [(1, 0)])
    lower = jnp.where(core == 1, halves[:, 1], sent)
    owner = ((x == 0) & (z == 0)).astype(jnp.int32).reshape(1)
    cross = [lower] + [lax.ppermute(lower, ("x", "z"), [(0, k * NZ)]) for k in range(1, NX)]

    place = jnp.arange(width)
    c_of, q_of, i_of = place // half, place % half // rows_local, place % rows_local
    natural = (q_of * NC + c_of) * rows_local + i_of
    order = (natural[:, None] == place[None, :]).astype(HALF)
    sizes = (n_blk, t, half, width)


    def ordered(value):
        return jnp.dot(value, order, preferred_element_type=WIDE).astype(HALF)

    def both_cores(value):
        pair = lax.all_gather(value, "core", axis=0, tiled=False)
        return jnp.concatenate([pair[0], pair[1]], axis=-1)

    planes = [inverse]
    for k in range(1, NZ):
        planes.append(lax.ppermute(inverse, "z", [(k, 0)]))

    def first_half(pivot, planes):
        partial = run_kernel(first_kernel, *sizes, (), pivot, *planes)
        first = scatter_sum(partial).astype(HALF)
        return first, lax.all_gather(first, "core", axis=0, tiled=False)

    def second_half(first, pair, pivot, planes, cross):
        kernel = functools.partial(cross_kernel, rows_local)
        partial = run_kernel(kernel, *sizes, (), owner, pair, *cross)
        pair = lax.all_gather(scatter_sum(partial), "core", axis=0, tiled=False)
        scratch = (pltpu.VMEM((t, width), HALF),)
        partial = run_kernel(second_kernel, *sizes, scratch, pivot, pair, *planes)
        return jnp.stack([first, scatter_sum(partial).astype(HALF)])

    def none_first(pivot, planes):
        return jnp.zeros((t, half), HALF), jnp.zeros((NC, t, half), HALF)

    def none_second(first, pair, pivot, planes, cross):
        return jnp.zeros((STEPS, t, half), HALF)

    first, pair = lax.cond(z == 0, first_half, none_first, pivot, planes)
    solved = lax.cond(
        z == 0, second_half, none_second, first, pair, pivot, planes, cross
    )

    solved, panels, row = lax.optimization_barrier((solved, panels, row))
    extra = 128
    pick = jnp.arange(extra)
    at = pick // rows_local * width + row % per_blk * rows_local + pick % rows_local
    wanted = (pick < STEPS * rows_local) & (row // per_blk == blk)
    select = wanted[:, None] & (at[:, None] == jnp.arange(STEPS * width)[None, :])
    select = select.astype(HALF)

    spread = solved
    for k in range(1, NZ):
        received = lax.ppermute(solved, "z", [(0, k)])
        spread = spread + received
    spread = ordered(both_cores(gather_by_swap(spread, "x", NX)))
    spread = spread.reshape(NX, STEPS, n_blk, dates_x, width).transpose(2, 0, 3, 1, 4)
    spread = spread.reshape(dates_local * n_blk, STEPS * width)

    panel = jnp.concatenate(
        [
            jnp.where(row > k, panels[k], jnp.zeros((), HALF))
            for k in range(STEPS)
        ],
        axis=1,
    )
    panel = jnp.concatenate([panel, select], axis=0)

    total = product(spread, panel).astype(HALF)
    lanes, rows8 = 128, 8
    total = total.reshape(n_blk * dates_local // rows8, rows8, -1, lanes).transpose(0, 2, 1, 3)
    total = swap_blocks(total.reshape(n_blk, -1, lanes), "blk")
    return pl.pallas_call(
        finish_kernel,
        out_shape=(
            jax.ShapeDtypeStruct((STEPS, dates_local, rows_local), WIDE),
            jax.ShapeDtypeStruct(right_side.shape, WIDE),
        ),
    )(total, right_side)


def solution(mesh):
    shape = (NX, NZ, NC, mesh.shape["blk"])
    fine = Mesh(mesh.devices.reshape(shape), ("x", "z", "core", "blk"))
    row = ("x", "z", "core")
    return jax.shard_map(
        local,
        mesh=fine,
        in_specs=(P(row, None, "blk"), P("blk", row), P(None, row, "blk")),
        out_specs=(P(None, "blk", row), P("blk", row)),
        check_vma=False,
    )
```
